32 devices in a mesh: stratum: 4 (over y, x), user: 8 (over z, core).
Axes of the slice: x: 2, y: 2, z: 4, core: 2. Of those that a mesh axis runs over, the one named last changes fastest.
Arguments:
- users: bfloat16 [32768, 512], P(('stratum', 'user')), may hold values from -6 to 6
- items: float32 [256, 512], P(('stratum', 'user')), may hold values from -6 to 6
- momentum: float32 [256, 512], P(('stratum', 'user')), may hold values from -30 to 30
- ratings: bfloat16 [32768, 4, 64], P(('stratum', 'user')), may hold values from -6.25 to 6.25, as said below
Outputs:
- new_users: bfloat16 [32768, 512], P(('stratum', 'user'))
- new_items: float32 [256, 512], P(('stratum', 'user'))
- new_momentum: float32 [256, 512], P(('stratum', 'user'))
The draws below stay inside these ranges and needn't reach their ends.
Inputs may be any that keep to these rules, and one draw needn't show every extreme that they name: `ratings`: an entry equal to zero marks an unobserved rating; every observed rating has magnitude 0.25 or more.
All inputs are finite; a program needn't handle non-finite values.
Results may differ from the reference program's by a relative error of at most 0.013.
The reference program's roundings to bfloat16 on the way count: a program that leaves them out, or rounds other values in their place, can miss the bound.
Values may be sent and summed in bfloat16 or wider, within the bound.
No kernel may reach another device: no remote copies, remote signals or barrier semaphores. Data moves between devices by JAX's collectives and lax.ppermute only.
A program may use at most 64 MiB of HBM per device.

```python
import jax
import jax.numpy as jnp
from jax import lax

R = 512
USR_DEV = 1024
ITEM_DEV = 8
STEPS = 4
ITEM_BLK = 64
USERS = 32768
ITEMS = 256
N_STRATUM = 4
N_USER = 8


def draw_ratings(key, part):
    keys = jax.random.split(jax.random.fold_in(key, 7), 4)
    row_factor = jax.random.uniform(keys[0], (USERS, 1, 1), jnp.float32, 0.55, 1.0)
    col_factor = jax.random.uniform(keys[1], (1, STEPS, ITEM_BLK), jnp.float32, 0.6, 1.0)
    chance = jax.random.uniform(keys[2], (USERS, STEPS, ITEM_BLK), jnp.float32)
    observed = chance < row_factor * col_factor
    normal = jnp.clip(jax.random.normal(keys[3], (USERS, STEPS, ITEM_BLK), jnp.float32), -6.0, 6.0)
    values = jnp.where(normal >= 0, 0.25 + normal, -0.25 + normal)
    return jnp.where(observed, values, 0.0).astype(jnp.bfloat16)


def block_levels(own_key, extent, cuts, smallest, high):
    def one(dim, shards_of):
        heights = jax.random.uniform(jax.random.fold_in(jax.random.fold_in(own_key, 6), dim), (shards_of,), jnp.float32, smallest / len(cuts), high / len(cuts))
        return jnp.repeat(jnp.exp(heights), extent[dim] // shards_of).reshape((-1,) + (1,) * (len(extent) - dim - 1))

    factor_of = one(*cuts[0])
    for cut in cuts[1:]:
        factor_of = factor_of * one(*cut)
    return factor_of


def scatter_about(own_key, shape, spread, most, cuts=(), dtype=jnp.bfloat16):
    loudness = block_levels(own_key, shape, cuts, -0.22, 0.18) if cuts else 1.0
    drawn = jax.random.normal(own_key, shape, jnp.float32) * spread * loudness
    return jnp.minimum(jnp.maximum(drawn, -most), most).astype(dtype)


def setup_inputs(seed: int = 0) -> dict:
    seeds = jax.random.split(jax.random.key(seed), 5)
    users = scatter_about(seeds[0], (USERS, R), 1.0, 6.0, ((0, 32),))
    items = scatter_about(seeds[1], (ITEMS, R), 1.0, 6.0, ((0, 32),), jnp.float32)
    momentum = scatter_about(seeds[2], (ITEMS, R), 5.0, 30.0, ((0, 32),), jnp.float32)
    ratings = draw_ratings(jax.random.fold_in(seeds[4], 71), 0)
    return {"users": users, "items": items, "momentum": momentum, "ratings": ratings}


user_rate = 1.0
item_rate = 0.04
inertia = 0.6


def reference(users, items, momentum, ratings):
    strata = N_STRATUM
    user_rows = USR_DEV * N_USER
    block_rows = ITEM_DEV * N_USER
    factor = R ** -0.5
    ublock = users.reshape(strata, user_rows, R)
    vblock = items.reshape(strata, block_rows, R)
    mblock = momentum.reshape(strata, block_rows, R)
    tiles = ratings.reshape(strata, user_rows, STEPS, block_rows)

    def one_stratum(packed):
        urows, vrows, tile = packed
        weights = vrows.astype(jnp.bfloat16)
        score = jnp.dot(urows, weights.T, preferred_element_type=jnp.float32)
        resid = jnp.where(tile != 0, score * factor - tile.astype(jnp.float32), 0.0).astype(jnp.bfloat16)
        grads = jnp.dot(resid.T, urows, preferred_element_type=jnp.float32)
        change = jnp.dot(resid, weights, preferred_element_type=jnp.float32)
        fresh = (urows.astype(jnp.float32) - user_rate * factor * change).astype(jnp.bfloat16)
        return fresh, grads

    for step in range(STEPS):
        ublock, grads = lax.map(one_stratum, (ublock, vblock, tiles[:, :, step, :]))
        mblock = inertia * mblock + factor * grads
        vblock = vblock - item_rate * mblock
        vblock = jnp.roll(vblock, -1, 0)
        mblock = jnp.roll(mblock, -1, 0)
    return ublock.reshape(USERS, R), vblock.reshape(ITEMS, R), mblock.reshape(ITEMS, R)
```

```python
import jax
import jax.numpy as jnp
from jax import lax
from jax.sharding import PartitionSpec as P


AXES = ("stratum", "user")
user_rate = 1.0
item_rate = 0.04
inertia = 0.6


def send(block, shift, flip):
    strata, users = lax.axis_size("stratum"), lax.axis_size("user")
    route = [
        (s * users + u, (s - shift) % strata * users + (u ^ flip))
        for s in range(strata)
        for u in range(users)
    ]
    return lax.ppermute(block, AXES, route)


def wide(block):
    return block.astype(jnp.float32)


def narrow(block):
    return block.astype(jnp.bfloat16)


def local(users, items, momentum, ratings):
    steps, rank = ratings.shape[1], users.shape[1]
    factor = rank ** (-0.5)
    own = items.shape[0]
    n = lax.axis_size("user")
    slices = n // 2
    top = n // 2
    me = lax.axis_index("user")
    core, place = me % 2, me // 2

    def half(block, which):
        parts = block.reshape(slices, 2, own, rank)
        return lax.dynamic_index_in_dim(parts, which, 1, keepdims=False).reshape(-1, rank)

    def slice_at(block, where):
        return lax.dynamic_slice_in_dim(block, where * own, own, 0)

    def gather_half(block):
        got = {0: block}
        for d in range(1, slices):
            got[d] = send(block, 0, 2 * d)
        stack = jnp.stack([got[d] for d in range(slices)])
        order = jnp.arange(slices) ^ place
        return jnp.take(stack, order, axis=0)

    def both(mine):
        other = send(mine, 0, 1)
        low = jnp.where(core == 0, mine, other).reshape(slices, own, rank)
        high = jnp.where(core == 0, other, mine).reshape(slices, own, rank)
        return jnp.stack([low, high], axis=1).reshape(-1, rank)

    state = gather_half(jnp.concatenate([items, momentum], axis=0).reshape(2, own, rank))
    value = state[:, 0].reshape(-1, rank)
    moment = state[:, 1].reshape(-1, rank)
    whole = both(narrow(value))
    for step in range(steps):
        last = step == steps - 1
        tile = ratings[:, step, :]
        score = lax.dot_general(
            users, whole, (((1,), (1,)), ((), ())), preferred_element_type=jnp.float32
        )
        resid = narrow(jnp.where(tile != 0, score * factor - wide(tile), 0.0))
        grads = lax.dot_general(
            resid, users, (((0,), (0,)), ((), ())), preferred_element_type=jnp.float32
        )
        keep, give = half(grads, core), narrow(half(grads, 1 - core))
        total = (
            keep
            + wide(send(give, 0, 1))
            + wide(send(narrow(keep), 0, 2))
            + wide(send(give, 0, 3))
        )
        bit = 4
        while bit < top:
            total = total + wide(send(narrow(total), 0, bit))
            bit *= 2
        total = narrow(total)
        if last:
            value, moment = slice_at(value, place), slice_at(moment, place)
            near = slice_at(total, place)
            far = slice_at(total, place ^ (top // 2))
        else:
            near = far = total
        value, moment = send(value, 1, 0), send(moment, 1, 0)
        grads = wide(send(near, 1, 0)) + wide(send(far, 1, top))
        change = jnp.dot(resid, whole, preferred_element_type=jnp.float32)
        users = narrow(wide(users) - user_rate * factor * change)
        moment = inertia * moment + factor * grads
        value = value - item_rate * moment
        if not last:
            whole = both(narrow(value))
    return users, value, moment


def solution(mesh):
    rows = P(AXES, None)
    return jax.shard_map(
        local,
        mesh=mesh,
        in_specs=(rows, rows, rows, P(AXES, None, None)),
        out_specs=(rows, rows, rows),
        check_vma=False,
    )
```

```python
import jax
import jax.numpy as jnp
from jax import lax
from jax.sharding import PartitionSpec as P


AXES = ("stratum", "user")
user_rate = 1.0
item_rate = 0.04
inertia = 0.6


def send(block, shift, flip):
    strata, users = lax.axis_size("stratum"), lax.axis_size("user")
    route = [
        (s * users + u, (s - shift) % strata * users + (u ^ flip))
        for s in range(strata)
        for u in range(users)
    ]
    return lax.ppermute(block, AXES, route)


def wide(block):
    return block.astype(jnp.float32)


def narrow(block):
    return block.astype(jnp.bfloat16)


def local(users, items, momentum, ratings):
    steps, rank = ratings.shape[1], users.shape[1]
    factor = rank ** (-0.5)
    own = items.shape[0]
    n = lax.axis_size("user")
    slices = n // 2
    top = n // 2
    me = lax.axis_index("user")
    core, place = me % 2, me // 2

    def half(block, which):
        parts = block.reshape(slices, 2, own, rank)
        return lax.dynamic_index_in_dim(parts, which, 1, keepdims=False).reshape(-1, rank)

    def slice_at(block, where):
        return lax.dynamic_slice_in_dim(block, where * own, own, 0)

    def gather_half(block):
        got = {0: block}
        for d in range(1, slices):
            got[d] = send(block, 0, 2 * d)
        bits = [place >> b & 1 for b in range((slices - 1).bit_length())]
        parts = [got[d] for d in range(slices)]
        for b, bit in enumerate(bits):
            parts = [jnp.where(bit == 1, parts[i ^ (1 << b)], parts[i]) for i in range(slices)]
        return jnp.concatenate(parts, axis=0)

    def both(mine, other):
        low = jnp.where(core == 0, mine, other).reshape(slices, own, rank)
        high = jnp.where(core == 0, other, mine).reshape(slices, own, rank)
        return jnp.stack([low, high], axis=1).reshape(-1, rank)

    value = gather_half(narrow(items))
    whole = both(value, send(value, 0, 1))
    share = [
        jnp.where(me == i, inertia * momentum, 0.0) for i in range(n)
    ]
    share = jnp.concatenate(share, axis=0)
    for step in range(steps):
        last = step == steps - 1
        tile = ratings[:, step, :]
        score = lax.dot_general(
            users, whole, (((1,), (1,)), ((), ())), preferred_element_type=jnp.float32
        )
        resid = narrow(jnp.where(tile != 0, score * factor - wide(tile), 0.0))
        grads = lax.dot_general(
            resid, users, (((0,), (0,)), ((), ())), preferred_element_type=jnp.float32
        )
        if step == 0:
            grads = factor * grads + share
            keep, give = half(grads, core), narrow(half(grads, 1 - core))
        else:
            keep = factor * half(grads, core) + share
            give = narrow(factor * half(grads, 1 - core))
        total = (
            keep
            + wide(send(give, 0, 1))
            + wide(send(narrow(keep), 0, 2))
            + wide(send(give, 0, 3))
        )
        bit = 4
        while bit < top:
            total = total + wide(send(narrow(total), 0, bit))
            bit *= 2
        total = narrow(total)
        near, far, kept = total, total, value
        if last:
            near, kept = slice_at(total, place), slice_at(value, place)
            far = slice_at(total, place ^ (top // 2))
        near = send(jnp.concatenate([near, kept], axis=0), 1, 0)
        far = send(far, 1, top)
        change = jnp.dot(resid, whole, preferred_element_type=jnp.float32)
        users = narrow(wide(users) - user_rate * factor * change)
        rows = far.shape[0]
        moment = wide(near[:rows]) + wide(far)
        fresh = wide(near[rows:]) - item_rate * moment
        if not last:
            value = narrow(fresh)
            whole = both(value, send(value, 0, 1))
            share = (inertia / slices) * moment
    return users, fresh, moment


def solution(mesh):
    rows = P(AXES, None)
    return jax.shard_map(
        local,
        mesh=mesh,
        in_specs=(rows, rows, rows, P(AXES, None, None)),
        out_specs=(rows, rows, rows),
        check_vma=False,
    )
```

```python
import jax
import jax.numpy as jnp
from jax import lax
from jax.sharding import PartitionSpec as P


AXES = ("stratum", "user")
user_rate = 1.0
item_rate = 0.04
inertia = 0.6


def wide(block):
    return block.astype(jnp.float32)


def narrow(block):
    return block.astype(jnp.bfloat16)


def route(block, target):
    strata, users = lax.axis_size("stratum"), lax.axis_size("user")
    pairs = []
    for s in range(strata):
        for u in range(users):
            there, who = target(s, u)
            pairs.append((s * users + u, there % strata * users + who))
    return lax.ppermute(block, AXES, pairs)


def swap(block, bits):
    return route(block, lambda s, u: (s, u ^ bits))


def even_to_odd(block, bits):
    return route(block, lambda s, u: (s, u ^ 1) if u % 2 else (s, u ^ bits ^ 1))


def odd_to_even_back(block, bits):
    return route(block, lambda s, u: (s - 1, u ^ bits ^ 1) if u % 2 else (s, u ^ 1))


def local(users, items, momentum, ratings):
    steps, rank = ratings.shape[1], users.shape[1]
    factor = rank ** (-0.5)
    own = items.shape[0]
    n = lax.axis_size("user")
    slices = n // 2
    top = n // 2
    me = lax.axis_index("user")
    core, place = me % 2, me // 2

    def chip_rows(block):
        return lax.dynamic_slice_in_dim(block, place * 2 * own, 2 * own, 0)

    mine = narrow(items)
    other = swap(mine, 1)
    pair = jnp.where(core == 0, jnp.stack([mine, other]), jnp.stack([other, mine]))
    pair = pair.reshape(2 * own, rank)
    parts = [pair] + [swap(pair, 2 * d) for d in range(1, slices)]
    for b in range((slices - 1).bit_length()):
        bit = place >> b & 1
        parts = [jnp.where(bit == 1, parts[i ^ (1 << b)], parts[i]) for i in range(slices)]
    whole = jnp.concatenate(parts, axis=0)

    owner = lax.broadcasted_iota(jnp.int32, (n, own, rank), 0)
    share = jnp.where(owner == me, inertia * momentum[None], 0.0).reshape(-1, rank)
    for step in range(steps):
        last = step == steps - 1
        tile = ratings[:, step, :]
        score = lax.dot_general(
            users, whole, (((1,), (1,)), ((), ())), preferred_element_type=jnp.float32
        )
        resid = narrow(jnp.where(tile != 0, score * factor - wide(tile), 0.0))
        grads = lax.dot_general(
            resid, users, (((0,), (0,)), ((), ())), preferred_element_type=jnp.float32
        )
        grads = factor * grads + share
        total = narrow(grads + wide(swap(narrow(grads), 1)))
        bit = 4
        while bit < top:
            total = narrow(wide(total) + wide(swap(total, bit)))
            bit *= 2
        total = narrow(wide(total) + wide(even_to_odd(total, 2)))
        if last:
            far = lax.dynamic_slice_in_dim(total, (place ^ (top // 2)) * 2 * own, 2 * own, 0)
            near = jnp.concatenate([chip_rows(total), chip_rows(whole)], axis=0)
        else:
            far, near = total, jnp.concatenate([total, whole], axis=0)
        far = odd_to_even_back(far, top)
        near = odd_to_even_back(near, 0)
        change = jnp.dot(resid, whole, preferred_element_type=jnp.float32)
        users = narrow(wide(users) - user_rate * factor * change)
        rows = far.shape[0]
        moment = wide(near[:rows]) + wide(far)
        fresh = wide(near[rows:]) - item_rate * moment
        if last:
            both = jnp.concatenate([fresh, moment], axis=0).reshape(2, 2, own, rank)
            got = swap(both[:, 1], 1)
            fresh, moment = jnp.where(core == 0, both[:, 0], got)
        else:
            fresh = narrow(fresh)
            whole = jnp.where(core == 0, fresh, swap(fresh, 1))
            share = jnp.where(core == 0, (inertia / slices) * moment, 0.0)
    return users, fresh, moment


def solution(mesh):
    rows = P(AXES, None)
    return jax.shard_map(
        local,
        mesh=mesh,
        in_specs=(rows, rows, rows, P(AXES, None, None)),
        out_specs=(rows, rows, rows),
        check_vma=False,
    )
```

```python
import jax
import jax.numpy as jnp
from jax import lax
from jax.sharding import PartitionSpec as P


AXES = ("stratum", "user")
user_rate = 1.0
item_rate = 0.04
inertia = 0.6


def wide(block):
    return block.astype(jnp.float32)


def narrow(block):
    return block.astype(jnp.bfloat16)


def route(block, target):
    strata, users = lax.axis_size("stratum"), lax.axis_size("user")
    pairs = []
    for s in range(strata):
        for u in range(users):
            there, who = target(s, u)
            pairs.append((s * users + u, there % strata * users + who))
    return lax.ppermute(block, AXES, pairs)


def swap(block, bits):
    return route(block, lambda s, u: (s, u ^ bits))


def even_to_odd(block, bits):
    return route(block, lambda s, u: (s, u ^ 1) if u % 2 else (s, u ^ bits ^ 1))


def odd_to_even_back(block, bits):
    return route(block, lambda s, u: (s - 1, u ^ bits ^ 1) if u % 2 else (s, u ^ 1))


def local(users, items, momentum, ratings):
    steps, rank = ratings.shape[1], users.shape[1]
    factor = rank ** (-0.5)
    own = items.shape[0]
    n = lax.axis_size("user")
    slices = n // 2
    top = n // 2
    me = lax.axis_index("user")
    core, place = me % 2, me // 2

    def in_order(mine, other, late):
        return jnp.concatenate(
            [jnp.where(late == 0, mine, other), jnp.where(late == 0, other, mine)], axis=0
        )

    def chip_rows(block):
        return lax.dynamic_slice_in_dim(block, place * 2 * own, 2 * own, 0)

    mine = narrow(items)
    block, bit = mine, 1
    while bit < top // 2:
        block = in_order(block, swap(block, bit), me // bit % 2)
        bit *= 2
    block = in_order(block, even_to_odd(block, bit), me // bit % 2)
    far = route(block, lambda s, u: (s, u ^ top ^ 1) if u % 2 else (s, u ^ 1))
    block = in_order(swap(block, 1), far, me // top)
    whole = jnp.where(core == 0, block, swap(block, 1))
    tiles = [ratings[:, step, :] for step in range(steps)]
    tiles[0] = lax.optimization_barrier(tiles[0])

    owner = lax.broadcasted_iota(jnp.int32, (n, own, rank), 0)
    share = jnp.where(owner == me, inertia * momentum[None], 0.0).reshape(-1, rank)
    for step in range(steps):
        last = step == steps - 1
        score = lax.dot_general(
            users, whole, (((1,), (1,)), ((), ())), preferred_element_type=jnp.float32
        )
        resid = narrow(jnp.where(tiles[step] != 0, score * factor - wide(tiles[step]), 0.0))
        grads = lax.dot_general(
            resid, users, (((0,), (0,)), ((), ())), preferred_element_type=jnp.float32
        )
        grads = factor * grads + share
        total = narrow(grads + wide(swap(narrow(grads), 1)))
        bit = 4
        while bit < top:
            total = narrow(wide(total) + wide(swap(total, bit)))
            bit *= 2
        value = chip_rows(whole) if last else whole
        other = even_to_odd(total, 2)
        value, _ = lax.optimization_barrier((value, total))
        value = odd_to_even_back(value, 0)
        total = narrow(wide(total) + wide(other))
        far, near = total, total
        if last:
            far = lax.dynamic_slice_in_dim(total, (place ^ (top // 2)) * 2 * own, 2 * own, 0)
            near = chip_rows(total)
        far = odd_to_even_back(far, top)
        near = odd_to_even_back(near, 0)
        change = jnp.dot(resid, whole, preferred_element_type=jnp.float32)
        users = narrow(wide(users) - user_rate * factor * change)
        moment = wide(near) + wide(far)
        fresh = wide(value) - item_rate * moment
        if last:
            both = jnp.concatenate([fresh, moment], axis=0).reshape(2, 2, own, rank)
            got = swap(both[:, 1], 1)
            fresh, moment = jnp.where(core == 0, both[:, 0], got)
        else:
            fresh = narrow(fresh)
            whole = jnp.where(core == 0, fresh, swap(fresh, 1))
            share = jnp.where(core == 0, (inertia / slices) * moment, 0.0)
    return users, fresh, moment


def solution(mesh):
    rows = P(AXES, None)
    return jax.shard_map(
        local,
        mesh=mesh,
        in_specs=(rows, rows, rows, P(AXES, None, None)),
        out_specs=(rows, rows, rows),
        check_vma=False,
    )
```

```python
import jax
import jax.numpy as jnp
from jax import lax
from jax.sharding import PartitionSpec as P


AXES = ("stratum", "user")
user_rate = 1.0
item_rate = 0.04
inertia = 0.6


def wide(block):
    return block.astype(jnp.float32)


def narrow(block):
    return block.astype(jnp.bfloat16)


def route(block, target):
    strata, users = lax.axis_size("stratum"), lax.axis_size("user")
    pairs = []
    for s in range(strata):
        for u in range(users):
            there, who = target(s, u)
            pairs.append((s * users + u, there % strata * users + who))
    return lax.ppermute(block, AXES, pairs)


def swap(block, bits):
    return route(block, lambda s, u: (s, u ^ bits))


def back(block, even, odd):
    return route(block, lambda s, u: (s - 1, u ^ (odd if u % 2 else even)))


def local(users, items, momentum, ratings):
    steps, rank = ratings.shape[1], users.shape[1]
    factor = rank ** (-0.5)
    own = items.shape[0]
    n = lax.axis_size("user")
    top = n // 2
    me = lax.axis_index("user")
    core, place = me % 2, me // 2

    def in_order(mine, other, late):
        return jnp.concatenate(
            [jnp.where(late == 0, mine, other), jnp.where(late == 0, other, mine)], axis=0
        )

    def rows_of(block, start, count):
        return lax.dynamic_slice_in_dim(block, start, count, 0)

    mine = lax.optimization_barrier(narrow(items))
    block, bit = mine, 1
    while bit < top // 2:
        block = in_order(block, swap(block, bit), me // bit % 2)
        bit *= 2
    near, far, cross = swap(block, bit), swap(block, top), swap(block, bit + top)
    side, end = me // bit % 2, me // top
    whole = in_order(in_order(block, near, side), in_order(far, cross, side), end)
    tiles = [ratings[:, step, :] for step in range(steps)]
    tiles[0] = lax.optimization_barrier(tiles[0])

    owner = lax.broadcasted_iota(jnp.int32, (n, own, rank), 0)
    share = jnp.where(owner == me, inertia * momentum[None], 0.0).reshape(-1, rank)
    for step in range(steps):
        last = step == steps - 1
        score = lax.dot_general(
            users, whole, (((1,), (1,)), ((), ())), preferred_element_type=jnp.float32
        )
        resid = narrow(jnp.where(tiles[step] != 0, score * factor - wide(tiles[step]), 0.0))
        grads = lax.dot_general(
            resid, users, (((0,), (0,)), ((), ())), preferred_element_type=jnp.float32
        )
        grads = factor * grads + share
        total, bit = narrow(grads), 1
        while bit < top // 2:
            grads = grads + wide(swap(total, bit))
            total = narrow(grads)
            bit *= 2
        first = (bit, top)
        second = (0, bit + top)

        def part(flip):
            return rows_of(total, (place ^ flip // 2) * 2 * own, 2 * own)

        def picked(flips):
            if not last:
                return total
            return jnp.where(core == 0, part(flips[0]), part(flips[1]))

        one = back(picked(first), *first)
        two = back(picked(second), *second)
        if last:
            value = rows_of(whole, me * own, own)
        else:
            value = rows_of(whole, core * (n // 2 * own), n // 2 * own)
        value = back(value, 0, 0)
        change = jnp.dot(resid, whole, preferred_element_type=jnp.float32)
        users = narrow(wide(users) - user_rate * factor * change)
        moment = wide(one) + wide(two)
        if last:
            give = rows_of(moment, (1 - core) * own, own)
            moment = rows_of(moment, core * own, own) + wide(swap(narrow(give), 1))
        else:
            moment = narrow(moment)
            moment = wide(moment) + wide(swap(moment, 1))
            value = in_order(value, swap(value, 1), core)
        fresh = wide(value) - item_rate * moment
        whole = narrow(fresh)
        share = (inertia / n) * moment
    return users, fresh, moment


def solution(mesh):
    rows = P(AXES, None)
    return jax.shard_map(
        local,
        mesh=mesh,
        in_specs=(rows, rows, rows, P(AXES, None, None)),
        out_specs=(rows, rows, rows),
        check_vma=False,
    )
```

```python
import jax
import jax.numpy as jnp
from jax import lax
from jax.sharding import PartitionSpec as P


AXES = ("stratum", "user")
user_rate = 1.0
item_rate = 0.04
inertia = 0.6


def wide(block):
    return block.astype(jnp.float32)


def narrow(block):
    return block.astype(jnp.bfloat16)


def route(block, target):
    strata, users = lax.axis_size("stratum"), lax.axis_size("user")
    pairs = []
    for s in range(strata):
        for u in range(users):
            there, who = target(s, u)
            pairs.append((s * users + u, there % strata * users + who))
    return lax.ppermute(block, AXES, pairs)


def swap(block, bits):
    return route(block, lambda s, u: (s, u ^ bits))


def back(block, even, odd):
    return route(block, lambda s, u: (s - 1, u ^ (odd if u % 2 else even)))


def local(users, items, momentum, ratings):
    steps, rank = ratings.shape[1], users.shape[1]
    factor = rank ** (-0.5)
    own = items.shape[0]
    n = lax.axis_size("user")
    top = n // 2
    me = lax.axis_index("user")
    core, place = me % 2, me // 2

    def in_order(mine, other, late):
        return jnp.concatenate(
            [jnp.where(late == 0, mine, other), jnp.where(late == 0, other, mine)], axis=0
        )

    def rows_of(block, start, count):
        return lax.dynamic_slice_in_dim(block, start, count, 0)

    block = narrow(items)
    block = in_order(block, swap(block, 1), core)
    one = jnp.ones((), users.dtype)
    block, shown, moving, one = lax.optimization_barrier((block, ratings, momentum, one))
    users = lax.optimization_barrier(users * one)
    bit = 2
    while bit < n:
        block = in_order(block, swap(block, bit), me // bit % 2)
        bit *= 2
    whole = lax.optimization_barrier(block)
    tiles = [ratings[:, step, :] for step in range(steps)]
    tiles[0] = lax.optimization_barrier(shown[:, 0, :])

    row = lax.broadcasted_iota(jnp.int32, (n * own, rank), 0) - me * own
    share = jnp.where((row >= 0) & (row < own), inertia * jnp.tile(moving, (n, 1)), 0.0)
    for step in range(steps):
        last = step == steps - 1
        score = lax.dot_general(
            users, whole, (((1,), (1,)), ((), ())), preferred_element_type=jnp.float32
        )
        resid = narrow(jnp.where(tiles[step] != 0, score * factor - wide(tiles[step]), 0.0))
        grads = lax.dot_general(
            resid, users, (((0,), (0,)), ((), ())), preferred_element_type=jnp.float32
        )
        grads = factor * grads + share
        total, bit = narrow(grads), 1
        while bit < top // 2:
            grads = grads + wide(swap(total, bit))
            total = narrow(grads)
            bit *= 2
        first = (bit, top)
        second = (0, bit + top)

        def part(flip):
            return rows_of(total, (place ^ flip // 2) * 2 * own, 2 * own)

        def picked(flips):
            if not last:
                return total
            return jnp.where(core == 0, part(flips[0]), part(flips[1]))

        one = back(picked(first), *first)
        two = back(picked(second), *second)
        if last:
            value = rows_of(whole, me * own, own)
        else:
            value = rows_of(whole, core * (n // 2 * own), n // 2 * own)
        value = back(value, 0, 0)
        change = jnp.dot(resid, whole, preferred_element_type=jnp.float32)
        users = narrow(wide(users) - user_rate * factor * change)
        moment = wide(one) + wide(two)
        if last:
            give = rows_of(moment, (1 - core) * own, own)
            moment = rows_of(moment, core * own, own) + wide(swap(narrow(give), 1))
        else:
            moment = narrow(moment)
            moment = wide(moment) + wide(swap(moment, 1))
            value = in_order(value, swap(value, 1), core)
        fresh = wide(value) - item_rate * moment
        whole = narrow(fresh)
        share = (inertia / n) * moment
    return users, fresh, moment


def solution(mesh):
    rows = P(AXES, None)
    return jax.shard_map(
        local,
        mesh=mesh,
        in_specs=(rows, rows, rows, P(AXES, None, None)),
        out_specs=(rows, rows, rows),
        check_vma=False,
    )
```

```python
import jax
import jax.numpy as jnp
from jax import lax
from jax.sharding import PartitionSpec as P


AXES = ("stratum", "user")
user_rate = 1.0
item_rate = 0.04
inertia = 0.6


def wide(block):
    return block.astype(jnp.float32)


def narrow(block):
    return block.astype(jnp.bfloat16)


def route(block, target):
    strata, users = lax.axis_size("stratum"), lax.axis_size("user")
    pairs = []
    for s in range(strata):
        for u in range(users):
            there, who = target(s, u)
            pairs.append((s * users + u, there % strata * users + who))
    return lax.ppermute(block, AXES, pairs)


def swap(block, bits):
    return route(block, lambda s, u: (s, u ^ bits))


def back(block, even, odd):
    return route(block, lambda s, u: (s - 1, u ^ (odd if u % 2 else even)))


def local(users, items, momentum, ratings):
    steps, rank = ratings.shape[1], users.shape[1]
    factor = rank ** (-0.5)
    own = items.shape[0]
    n = lax.axis_size("user")
    top = n // 2
    me = lax.axis_index("user")
    core, place = me % 2, me // 2

    def in_order(mine, other, late):
        return jnp.concatenate(
            [jnp.where(late == 0, mine, other), jnp.where(late == 0, other, mine)], axis=0
        )

    def rows_of(block, start, count):
        return lax.dynamic_slice_in_dim(block, start, count, 0)

    block = lax.optimization_barrier(narrow(items))
    block = in_order(block, swap(block, 1), core)
    one = jnp.ones((), users.dtype)
    block, shown, moving, one = lax.optimization_barrier((block, ratings, momentum, one))
    users = lax.optimization_barrier(users * one)
    bit = 2
    while bit < top // 2:
        block = in_order(block, swap(block, bit), me // bit % 2)
        bit *= 2
    near = swap(block, bit)
    far = swap(block, top)
    cross = swap(block, bit + top)
    side, end = me // bit % 2, me // top
    whole = in_order(in_order(block, near, side), in_order(far, cross, side), end)
    whole = lax.optimization_barrier(whole)
    tiles = [ratings[:, step, :] for step in range(steps)]
    tiles[0] = lax.optimization_barrier(shown[:, 0, :])

    row = lax.broadcasted_iota(jnp.int32, (n * own, rank), 0) - me * own
    share = jnp.where((row >= 0) & (row < own), inertia * jnp.tile(moving, (n, 1)), 0.0)
    for step in range(steps):
        last = step == steps - 1
        score = lax.dot_general(
            users, whole, (((1,), (1,)), ((), ())), preferred_element_type=jnp.float32
        )
        resid = narrow(jnp.where(tiles[step] != 0, score * factor - wide(tiles[step]), 0.0))
        grads = lax.dot_general(
            resid, users, (((0,), (0,)), ((), ())), preferred_element_type=jnp.float32
        )
        grads = factor * grads + share
        total, bit = narrow(grads), 1
        while bit < top // 2:
            grads = grads + wide(swap(total, bit))
            total = narrow(grads)
            bit *= 2
        first = (0, top)
        second = (bit, bit + top)

        def part(flip):
            return rows_of(total, (place ^ flip // 2) * 2 * own, 2 * own)

        def picked(flips):
            if not last:
                return total
            return jnp.where(core == 0, part(flips[0]), part(flips[1]))

        one = back(picked(first), *first)
        two = back(picked(second), *second)
        if last:
            value = rows_of(whole, me * own, own)
        else:
            value = whole
        value = back(value, 0, 0)
        change = jnp.dot(resid, whole, preferred_element_type=jnp.float32)
        users = narrow(wide(users) - user_rate * factor * change)
        moment = wide(one) + wide(two)
        if last:
            give = rows_of(moment, (1 - core) * own, own)
            moment = rows_of(moment, core * own, own) + wide(swap(narrow(give), 1))
        else:
            moment = narrow(moment)
            moment = wide(moment) + wide(swap(moment, 1))
        fresh = wide(value) - item_rate * moment
        whole = narrow(fresh)
        share = (inertia / n) * moment
    return users, fresh, moment


def solution(mesh):
    rows = P(AXES, None)
    return jax.shard_map(
        local,
        mesh=mesh,
        in_specs=(rows, rows, rows, P(AXES, None, None)),
        out_specs=(rows, rows, rows),
        check_vma=False,
    )
```

```python
import jax
import jax.numpy as jnp
from jax import lax
from jax.sharding import PartitionSpec as P


AXES = ("stratum", "user")
user_rate = 1.0
item_rate = 0.04
inertia = 0.6


def wide(block):
    return block.astype(jnp.float32)


def narrow(block):
    return block.astype(jnp.bfloat16)


def route(block, target):
    strata, users = lax.axis_size("stratum"), lax.axis_size("user")
    pairs = []
    for s in range(strata):
        for u in range(users):
            there, who = target(s, u)
            pairs.append((s * users + u, there % strata * users + who))
    return lax.ppermute(block, AXES, pairs)


def swap(block, bits):
    return route(block, lambda s, u: (s, u ^ bits))


def back(block, even, odd):
    return route(block, lambda s, u: (s - 1, u ^ (odd if u % 2 else even)))


def local(users, items, momentum, ratings):
    steps, rank = ratings.shape[1], users.shape[1]
    factor = rank ** (-0.5)
    own = items.shape[0]
    n = lax.axis_size("user")
    top = n // 2
    me = lax.axis_index("user")
    core, place = me % 2, me // 2

    def in_order(mine, other, late):
        return jnp.concatenate(
            [jnp.where(late == 0, mine, other), jnp.where(late == 0, other, mine)], axis=0
        )

    def rows_of(block, start, count):
        return lax.dynamic_slice_in_dim(block, start, count, 0)

    block = lax.optimization_barrier(narrow(items))
    block = in_order(block, swap(block, 1), core)
    one = jnp.ones((), users.dtype)
    block, shown, moving, one = lax.optimization_barrier((block, ratings, momentum, one))
    users = lax.optimization_barrier(users * one)
    bit = 2
    while bit < top // 2:
        block = in_order(block, swap(block, bit), me // bit % 2)
        bit *= 2
    got = route(block, lambda s, u: (s, u ^ (top if u % 2 else bit)))
    more = route(block, lambda s, u: (s, u ^ (bit + top if u % 2 else bit)))
    both = jnp.concatenate([got, more], axis=0)
    other = swap(both, 1)
    rows = block.shape[0]
    near = jnp.where(core == 0, got, other[:rows])
    far = jnp.where(core == 0, other[:rows], got)
    cross = jnp.where(core == 0, other[rows:], more)
    side, end = me // bit % 2, me // top
    whole = in_order(in_order(block, near, side), in_order(far, cross, side), end)
    whole = lax.optimization_barrier(whole)
    tiles = [ratings[:, step, :] for step in range(steps)]
    tiles[0] = lax.optimization_barrier(shown[:, 0, :])

    row = lax.broadcasted_iota(jnp.int32, (n * own, rank), 0) - me * own
    share = jnp.where((row >= 0) & (row < own), inertia * jnp.tile(moving, (n, 1)), 0.0)
    for step in range(steps):
        last = step == steps - 1
        score = lax.dot_general(
            users, whole, (((1,), (1,)), ((), ())), preferred_element_type=jnp.float32
        )
        resid = narrow(jnp.where(tiles[step] != 0, score * factor - wide(tiles[step]), 0.0))
        grads = lax.dot_general(
            resid, users, (((0,), (0,)), ((), ())), preferred_element_type=jnp.float32
        )
        grads = factor * grads + share
        total, bit = narrow(grads), 1
        while bit < top // 2:
            grads = grads + wide(swap(total, bit))
            total = narrow(grads)
            bit *= 2
        first = (0, top)
        second = (bit, bit + top)

        def part(flip):
            return rows_of(total, (place ^ flip // 2) * 2 * own, 2 * own)

        def picked(flips):
            if not last:
                return total
            return jnp.where(core == 0, part(flips[0]), part(flips[1]))

        one = back(picked(first), *first)
        two = back(picked(second), *second)
        if last:
            value = rows_of(whole, me * own, own)
        else:
            value = whole
        value = back(value, 0, 0)
        change = jnp.dot(resid, whole, preferred_element_type=jnp.float32)
        users = narrow(wide(users) - user_rate * factor * change)
        moment = wide(one) + wide(two)
        if last:
            give = rows_of(moment, (1 - core) * own, own)
            moment = rows_of(moment, core * own, own) + wide(swap(narrow(give), 1))
        else:
            moment = narrow(moment)
            moment = wide(moment) + wide(swap(moment, 1))
        fresh = wide(value) - item_rate * moment
        whole = narrow(fresh)
        share = (inertia / n) * moment
    return users, fresh, moment


def solution(mesh):
    rows = P(AXES, None)
    return jax.shard_map(
        local,
        mesh=mesh,
        in_specs=(rows, rows, rows, P(AXES, None, None)),
        out_specs=(rows, rows, rows),
        check_vma=False,
    )
```

```python
import jax
import jax.numpy as jnp
from jax import lax
from jax.sharding import PartitionSpec as P


AXES = ("stratum", "user")
user_rate = 1.0
item_rate = 0.04
inertia = 0.6


def wide(block):
    return block.astype(jnp.float32)


def narrow(block):
    return block.astype(jnp.bfloat16)


def route(block, target):
    strata, users = lax.axis_size("stratum"), lax.axis_size("user")
    pairs = []
    for s in range(strata):
        for u in range(users):
            there, who = target(s, u)
            pairs.append((s * users + u, there % strata * users + who))
    return lax.ppermute(block, AXES, pairs)


def swap(block, bits):
    return route(block, lambda s, u: (s, u ^ bits))


def back(block, even, odd):
    return route(block, lambda s, u: (s - 1, u ^ (odd if u % 2 else even)))


def local(users, items, momentum, ratings):
    steps, rank = ratings.shape[1], users.shape[1]
    factor = rank ** (-0.5)
    own = items.shape[0]
    n = lax.axis_size("user")
    top = n // 2
    me = lax.axis_index("user")
    core, place = me % 2, me // 2

    def in_order(mine, other, late):
        return jnp.concatenate(
            [jnp.where(late == 0, mine, other), jnp.where(late == 0, other, mine)], axis=0
        )

    def rows_of(block, start, count):
        return lax.dynamic_slice_in_dim(block, start, count, 0)

    block = lax.optimization_barrier(narrow(items))
    block = in_order(block, swap(block, 1), core)
    one = jnp.ones((), users.dtype)
    block, shown, moving, one = lax.optimization_barrier((block, ratings, momentum, one))
    users = lax.optimization_barrier(users * one)
    bit = 2
    while bit < top // 2:
        block = in_order(block, swap(block, bit), me // bit % 2)
        bit *= 2
    got = route(block, lambda s, u: (s, u ^ (top if u % 2 else bit)))
    more = route(block, lambda s, u: (s, u ^ (bit + top if u % 2 else bit)))
    both = jnp.concatenate([got, more], axis=0)
    other = swap(both, 1)
    rows = block.shape[0]
    near = jnp.where(core == 0, got, other[:rows])
    far = jnp.where(core == 0, other[:rows], got)
    cross = jnp.where(core == 0, other[rows:], more)
    side, end = me // bit % 2, me // top
    whole = in_order(in_order(block, near, side), in_order(far, cross, side), end)
    tiles = [ratings[:, step, :] for step in range(steps)]
    tiles[0] = lax.optimization_barrier(shown[:, 0, :])

    row = lax.broadcasted_iota(jnp.int32, (n * own, rank), 0) - me * own
    share = jnp.where((row >= 0) & (row < own), inertia * jnp.tile(moving, (n, 1)), 0.0)
    for step in range(steps):
        last = step == steps - 1
        score = lax.dot_general(
            users, whole, (((1,), (1,)), ((), ())), preferred_element_type=jnp.float32
        )
        resid = narrow(jnp.where(tiles[step] != 0, score * factor - wide(tiles[step]), 0.0))
        grads = lax.dot_general(
            resid, users, (((0,), (0,)), ((), ())), preferred_element_type=jnp.float32
        )
        grads = factor * grads + share
        total, bit = narrow(grads), 1
        while bit < top // 2:
            grads = grads + wide(swap(total, bit))
            total = narrow(grads)
            bit *= 2
        first = (0, top) if not last else (bit, top)
        second = (bit, bit + top) if not last else (0, bit + top)

        def part(flip):
            return rows_of(total, (place ^ flip // 2) * 2 * own, 2 * own)

        def picked(flips):
            if not last:
                return total
            return jnp.where(core == 0, part(flips[0]), part(flips[1]))

        one = back(picked(first), *first)
        two = back(picked(second), *second)
        if last:
            value = rows_of(whole, me * own, own)
        else:
            value = whole
        value = back(value, 0, 0)
        change = jnp.dot(resid, whole, preferred_element_type=jnp.float32)
        users = narrow(wide(users) - user_rate * factor * change)
        moment = wide(one) + wide(two)
        if last:
            give = rows_of(moment, (1 - core) * own, own)
            moment = rows_of(moment, core * own, own) + wide(swap(narrow(give), 1))
        else:
            moment = narrow(moment)
            moment = wide(moment) + wide(swap(moment, 1))
        fresh = wide(value) - item_rate * moment
        whole = narrow(fresh)
        share = (inertia / n) * moment
    return users, fresh, moment


def solution(mesh):
    rows = P(AXES, None)
    return jax.shard_map(
        local,
        mesh=mesh,
        in_specs=(rows, rows, rows, P(AXES, None, None)),
        out_specs=(rows, rows, rows),
        check_vma=False,
    )
```
